32 devices in a mesh: gx: 4 (over z), gy: 2 (over y), gz: 4 (over x, core).
Axes of the slice: x: 2, y: 2, z: 4, core: 2. Of those that a mesh axis runs over, the one named last changes fastest.
Arguments:
- displ: float32 [3, 4, 2, 4, 9945], P(None, 'gx', 'gy', 'gz'), may hold values from -6 to 6
- veloc: float32 [3, 4, 2, 4, 9945], P(None, 'gx', 'gy', 'gz'), may hold values from -6 to 6
- accel: float32 [3, 4, 2, 4, 9945], P(None, 'gx', 'gy', 'gz'), may hold values from -12 to 12
- node_index: int32 [4, 2, 4, 125, 128], P('gx', 'gy', 'gz'), may hold values from 0 to 9944, as said below
- inv_map: float32 [4, 2, 4, 9, 125, 128], P('gx', 'gy', 'gz'), may hold values from -1 to 2, as said below
- jac_weight: float32 [4, 2, 4, 125, 128], P('gx', 'gy', 'gz'), may hold values from 0.05 to 0.5
- lame_first: float32 [4, 2, 4, 125, 128], P('gx', 'gy', 'gz'), may hold values from 0.02 to 0.1
- shear_mod: float32 [4, 2, 4, 125, 128], P('gx', 'gy', 'gz'), may hold values from 0.02 to 0.1
- density: float32 [4, 2, 4, 125, 128], P('gx', 'gy', 'gz'), may hold values from 1 to 3
Outputs:
- displ_out: float32 [3, 4, 2, 4, 9945], P(None, 'gx', 'gy', 'gz')
- veloc_out: float32 [3, 4, 2, 4, 9945], P(None, 'gx', 'gy', 'gz')
- accel_out: float32 [3, 4, 2, 4, 9945], P(None, 'gx', 'gy', 'gz')
The draws below stay inside these ranges and needn't reach their ends.
Inputs may be any that keep to these rules, and one draw needn't show every extreme that they name: `node_index`: on each device the element slots hold the elements of a brick of 4 x 16 x 2 elements in a drawn order, each once; element (ex, ey, ez) has its point (a, b, c) at node ((4 ex + a) * 65 + 4 ey + b) * 9 + 4 ez + c. `inv_map`: the entries with l equal to j are positive.
All inputs are finite; a program needn't handle non-finite values.
Results may differ from the reference program's by a relative error of at most 0.00024.
Values sent between devices are 32-bit elements; how exact they have to be, the bound alone decides.
A program may use at most 64 MiB of HBM per device.

```python
import math
import jax
import jax.numpy as jnp
import numpy as np
from jax import lax

NGLL = 5
EX = 4
EY = 16
EZ = 2
STEPS = 1
E_DEV = 128
NODES_DEV = 9945
N_GX = 4
N_GY = 2
N_GZ = 4


def draw_node_index(key, part):
    devices = N_GX * N_GY * N_GZ
    elements = EX * EY * EZ
    keys = jax.random.split(key, devices)
    orders = jax.vmap(lambda subkey: jax.random.permutation(subkey, elements))(keys).astype(jnp.int32)
    elem_x = orders // (EY * EZ)
    elem_y = orders // EZ % EY
    elem_z = orders % EZ
    points = jnp.arange(125, dtype=jnp.int32)
    offset_a = points // 25
    offset_b = points // 5 % 5
    offset_c = points % 5
    node_y = 4 * EY + 1
    node_z = 4 * EZ + 1
    along_x = 4 * elem_x[:, None, :] + offset_a[None, :, None]
    along_y = 4 * elem_y[:, None, :] + offset_b[None, :, None]
    along_z = 4 * elem_z[:, None, :] + offset_c[None, :, None]
    flat = (along_x * node_y + along_y) * node_z + along_z
    return flat.reshape(N_GX, N_GY, N_GZ, 125, elements).astype(jnp.int32)


def draw_inv_map(key, part):
    elements = EX * EY * EZ
    shape = (N_GX, N_GY, N_GZ, 3, 3, 125, elements)
    diag_key, other_key = jax.random.split(key)
    diagonal = jax.random.uniform(diag_key, shape, jnp.float32, 0.7, 1.4)
    offdiag = jnp.clip(0.25 * jax.random.normal(other_key, shape, jnp.float32), -1.0, 1.0)
    identity = jnp.eye(3, dtype=jnp.float32)[:, :, None, None]
    full = identity * diagonal + (1.0 - identity) * offdiag
    return full.reshape(N_GX, N_GY, N_GZ, 9, 125, elements).astype(jnp.float32)


def block_levels(stream_key, dims, pieces, low, largest):
    loudness, own = 1.0, jax.random.fold_in(stream_key, 6)
    for axis_at, blocks in pieces:
        draws = jnp.exp(jax.random.uniform(jax.random.fold_in(own, axis_at), (blocks,), jnp.float32, low / len(pieces), largest / len(pieces)))
        loudness = loudness * jnp.repeat(draws, dims[axis_at] // blocks).reshape([-1 if axis == axis_at else 1 for axis in range(len(dims))])
    return loudness


def normal_values(key, extent, width, limit, shards=(), kind=jnp.bfloat16):
    values = width * jax.random.normal(key, extent, jnp.float32)
    if shards:
        values = values * block_levels(key, extent, shards, -0.22, 0.18)
    return jnp.clip(values, -limit, limit).astype(kind)


def setup_inputs(seed: int = 0) -> dict:
    seeds = jax.random.split(jax.random.key(seed), 10)
    return {
        "displ": normal_values(seeds[0], (3, N_GX, N_GY, N_GZ, NODES_DEV), 1.0, 6.0, ((1, 4), (2, 2), (3, 4)), jnp.float32),
        "veloc": normal_values(seeds[1], (3, N_GX, N_GY, N_GZ, NODES_DEV), 1.0, 6.0, ((1, 4), (2, 2), (3, 4)), jnp.float32),
        "accel": normal_values(seeds[2], (3, N_GX, N_GY, N_GZ, NODES_DEV), 2.0, 12.0, ((1, 4), (2, 2), (3, 4)), jnp.float32),
        "node_index": draw_node_index(jax.random.fold_in(seeds[9], 71), 0),
        "inv_map": draw_inv_map(jax.random.fold_in(seeds[9], 71), 0),
        "jac_weight": jnp.clip(jnp.exp(math.log(0.5) - 2.3025851 * jax.random.uniform(seeds[5], (N_GX, N_GY, N_GZ, NGLL * NGLL * NGLL, E_DEV), jnp.float32) ** block_levels(seeds[5], (N_GX, N_GY, N_GZ, NGLL * NGLL * NGLL, E_DEV), ((0, 4), (1, 2), (2, 4)), -0.2, 0.2)), 0.05, 0.5),
        "lame_first": jnp.clip(jnp.exp(math.log(0.1) - 1.609438 * jax.random.uniform(seeds[6], (N_GX, N_GY, N_GZ, NGLL * NGLL * NGLL, E_DEV), jnp.float32) ** block_levels(seeds[6], (N_GX, N_GY, N_GZ, NGLL * NGLL * NGLL, E_DEV), ((0, 4), (1, 2), (2, 4)), -0.2, 0.2)), 0.02, 0.1),
        "shear_mod": jnp.clip(jnp.exp(math.log(0.1) - 1.609438 * jax.random.uniform(seeds[7], (N_GX, N_GY, N_GZ, NGLL * NGLL * NGLL, E_DEV), jnp.float32) ** block_levels(seeds[7], (N_GX, N_GY, N_GZ, NGLL * NGLL * NGLL, E_DEV), ((0, 4), (1, 2), (2, 4)), -0.2, 0.2)), 0.02, 0.1),
        "density": jnp.clip(jnp.exp(math.log(3.0) - 1.0986123 * jax.random.uniform(seeds[8], (N_GX, N_GY, N_GZ, NGLL * NGLL * NGLL, E_DEV), jnp.float32) ** block_levels(seeds[8], (N_GX, N_GY, N_GZ, NGLL * NGLL * NGLL, E_DEV), ((0, 4), (1, 2), (2, 4)), -0.2, 0.2)), 1.0, 3.0),
    }


time_step = 0.1

def derivative_table():
    points = np.array([-1.0, -np.sqrt(3.0 / 7.0), 0.0, np.sqrt(3.0 / 7.0), 1.0])
    points_count = points.shape[0]
    weights = np.array([1.0 / np.prod([points[source] - points[other] for other in range(points_count) if other != source]) for source in range(points_count)])
    deriv_table = np.zeros((points_count, points_count))
    for target in range(points_count):
        for source in range(points_count):
            if target != source:
                deriv_table[target, source] = weights[source] / weights[target] / (points[target] - points[source])
        deriv_table[target, target] = -np.sum(deriv_table[target])
    return deriv_table

def element_force(position, node_index, inv_map, jac_weight, lame_first, shear_mod, deriv):
    highest = lax.Precision.HIGHEST
    elements = node_index.shape[1]
    nodes = position.shape[1]
    local = position[:, node_index].reshape(3, 5, 5, 5, elements)
    grad_a = jnp.einsum('ap,cpbke->cabke', deriv, local, precision=highest).reshape(3, 125, elements)
    grad_b = jnp.einsum('bp,capke->cabke', deriv, local, precision=highest).reshape(3, 125, elements)
    grad_c = jnp.einsum('kp,cabpe->cabke', deriv, local, precision=highest).reshape(3, 125, elements)
    mapping = inv_map.reshape(3, 3, 125, elements)
    strain_grad = grad_a[:, None] * mapping[0][None] + grad_b[:, None] * mapping[1][None] + grad_c[:, None] * mapping[2][None]
    divergence = strain_grad[0, 0] + strain_grad[1, 1] + strain_grad[2, 2]
    identity = jnp.eye(3, dtype=jnp.float32)[:, :, None, None]
    stress = shear_mod * (strain_grad + jnp.swapaxes(strain_grad, 0, 1)) + lame_first * divergence * identity
    flux = stress[:, 0][:, None] * mapping[:, 0][None] + stress[:, 1][:, None] * mapping[:, 1][None] + stress[:, 2][:, None] * mapping[:, 2][None]
    flux = (jac_weight * flux).reshape(3, 3, 5, 5, 5, elements)
    terms = jnp.einsum('pa,cpbke->cabke', deriv, flux[:, 0], precision=highest)
    terms = terms + jnp.einsum('pb,capke->cabke', deriv, flux[:, 1], precision=highest)
    terms = terms + jnp.einsum('pk,cabpe->cabke', deriv, flux[:, 2], precision=highest)
    return jnp.zeros((3, nodes), jnp.float32).at[:, node_index].add(-terms.reshape(3, 125, elements))

def fold_planes(field, dev_axis, node_axis):
    length = field.shape[node_axis]
    devices = field.shape[dev_axis]
    first = lax.slice_in_dim(field, 0, 1, axis=node_axis)
    last = lax.slice_in_dim(field, length - 1, length, axis=node_axis)
    middle = lax.slice_in_dim(field, 1, length - 1, axis=node_axis)
    zero_plane = jnp.zeros_like(lax.slice_in_dim(first, 0, 1, axis=dev_axis))
    from_lower = jnp.concatenate([zero_plane, lax.slice_in_dim(last, 0, devices - 1, axis=dev_axis)], axis=dev_axis)
    from_upper = jnp.concatenate([lax.slice_in_dim(first, 1, devices, axis=dev_axis), zero_plane], axis=dev_axis)
    return jnp.concatenate([first + from_lower, middle, last + from_upper], axis=node_axis)

def assemble_all(field):
    for dev_axis, node_axis in ((1, 4), (2, 5), (3, 6)):
        field = fold_planes(field, dev_axis, node_axis)
    return field

def reference(displ, veloc, accel, node_index, inv_map, jac_weight, lame_first, shear_mod, density):
    devices = N_GX * N_GY * N_GZ
    node_x = 4 * EX + 1
    node_y = 4 * EY + 1
    node_z = 4 * EZ + 1
    nodes = node_x * node_y * node_z
    elements = EX * EY * EZ
    deriv = jnp.asarray(derivative_table(), jnp.float32)
    index_all = node_index.reshape(devices, 125, elements)
    map_all = inv_map.reshape(devices, 9, 125, elements)
    weight_all = jac_weight.reshape(devices, 125, elements)
    lame_all = lame_first.reshape(devices, 125, elements)
    shear_all = shear_mod.reshape(devices, 125, elements)
    dens_all = density.reshape(devices, 125, elements)

    def mass_one(items):
        index, weight, dens = items
        return jnp.zeros((nodes,), jnp.float32).at[index].add(dens * weight)
    mass_local = lax.map(mass_one, (index_all, weight_all, dens_all))
    mass = assemble_all(mass_local.reshape(1, N_GX, N_GY, N_GZ, node_x, node_y, node_z))
    mass = mass.reshape(N_GX, N_GY, N_GZ, nodes)

    def force_one(items):
        position, index, mapping, weight, lame, shear = items
        return element_force(position, index, mapping, weight, lame, shear, deriv)
    half_step = 0.5 * time_step
    half_square = 0.5 * time_step * time_step
    for step in range(STEPS):
        displ = displ + time_step * veloc + half_square * accel
        veloc = veloc + half_step * accel
        moved = jnp.moveaxis(displ.reshape(3, devices, nodes), 1, 0)
        forces = lax.map(force_one, (moved, index_all, map_all, weight_all, lame_all, shear_all))
        forces = jnp.moveaxis(forces, 0, 1).reshape(3, N_GX, N_GY, N_GZ, node_x, node_y, node_z)
        forces = assemble_all(forces).reshape(3, N_GX, N_GY, N_GZ, nodes)
        accel = forces / mass[None]
        veloc = veloc + half_step * accel
    return (displ, veloc, accel)
```

```python
import jax
import jax.numpy as jnp
import numpy as np
from jax import lax
from jax.experimental import pallas as pl
from jax.experimental.pallas import tpu as pltpu
from jax.sharding import PartitionSpec as P

EX = 4
EY = 16
EZ = 2
NX = 4 * EX + 1
NY = 4 * EY + 1
NZ = 4 * EZ + 1
PLANE = NY * NZ
GROUP = 4
GROUPS = EY // GROUP
STEP = 4 * GROUP * NZ
SPAN = 256
WIDE = 640
GROW = 64
SROW = 72
SUB = EZ * GROUP

time_step = 0.1
MESH = pl.DeviceIdType.MESH


def derivative_table():
    points = np.array([-1.0, -np.sqrt(3.0 / 7.0), 0.0, np.sqrt(3.0 / 7.0), 1.0])
    count = points.shape[0]
    weights = np.array(
        [
            1.0 / np.prod([points[s] - points[o] for o in range(count) if o != s])
            for s in range(count)
        ]
    )
    table = np.zeros((count, count))
    for t in range(count):
        for s in range(count):
            if t != s:
                table[t, s] = weights[s] / weights[t] / (points[t] - points[s])
        table[t, t] = -np.sum(table[t])
    return table


def constants():
    table = derivative_table()
    select = np.zeros((25 * SUB, SPAN), np.float32)
    for b in range(5):
        for c in range(5):
            for ez in range(EZ):
                for ey in range(GROUP):
                    row = (b * 5 + c) * SUB + ez * GROUP + ey
                    select[row, (4 * ey + b) * NZ + 4 * ez + c] = 1.0
    eye = np.eye(5)
    parts = [
        np.kron(table, np.kron(eye, eye)),
        np.kron(eye, np.kron(table, eye)),
        np.kron(eye, np.kron(eye, table)),
    ]
    pad = np.zeros((125, 160))
    for a in range(5):
        for q in range(25):
            pad[a * 25 + q, a * 32 + q] = 1.0
    deriv = np.zeros((384, 160), np.float32)
    for l in range(3):
        deriv[l * 128 : l * 128 + 125] = parts[l] @ pad
    spread = np.zeros((160, 128), np.float32)
    spread[:, :125] = pad.T
    return select, deriv, -deriv.T.copy(), spread


def split3(x):
    hi = x.astype(jnp.bfloat16)
    rest = x - hi.astype(jnp.float32)
    mid = rest.astype(jnp.bfloat16)
    low = (rest - mid.astype(jnp.float32)).astype(jnp.bfloat16)
    return (hi, mid, low)


def dots(x, y, dims, split_left):
    total = None
    for piece in split3(x if split_left else y):
        left, right = (piece, y) if split_left else (x, piece)
        out = lax.dot_general(
            left, right, (dims, ((), ())), preferred_element_type=jnp.float32
        )
        total = out if total is None else total + out
    return total


def kernel(
    displ, veloc, accel, node, inv, jac, lame, shear, dens,
    select_ref, deriv_ref, back_ref, spread_ref,
    pos_out, spd_out, acc_out,
    d_s, v_s, a_s, node_s, inv_s, jac_s, lame_s, shear_s, dens_s,
    nf, u_s, fl_s, md_s, zp_s, grid_s, acc_s,
    z_send, z_recv, y_send, y_recv, x_send, x_recv,
    in_sem, out_sem, send_sem, recv_sem,
):
    names = ("gz", "gy", "gx")
    spots = [lax.axis_index(n) for n in names]
    sizes = [lax.axis_size(n) for n in names]
    has_low = [s > 0 for s in spots]
    has_high = [s < n - 1 for s, n in zip(spots, sizes)]
    barrier = pltpu.get_barrier_semaphore()
    for n, s, lo, hi in zip(names, spots, has_low, has_high):

        @pl.when(lo)
        def _():
            pl.semaphore_signal(barrier, inc=1, device_id={n: s - 1}, device_id_type=MESH)

        @pl.when(hi)
        def _():
            pl.semaphore_signal(barrier, inc=1, device_id={n: s + 1}, device_id_type=MESH)

    copies = []
    for k, (src, dst) in enumerate(((displ, d_s), (veloc, v_s), (accel, a_s))):
        for c in range(3):
            copies.append(
                pltpu.make_async_copy(
                    src.at[c], dst.at[pl.ds(c, 1)], in_sem.at[3 * k + c]
                )
            )
    elems = ((node, node_s), (inv, inv_s), (jac, jac_s), (lame, lame_s), (shear, shear_s), (dens, dens_s))
    for k, (src, dst) in enumerate(elems):
        copies.append(pltpu.make_async_copy(ELEM_SRC(src), dst, in_sem.at[9 + k]))
    for cp in copies:
        cp.start()
    nf[...] = jnp.zeros_like(nf)
    u_s[...] = jnp.zeros_like(u_s)
    fl_s[...] = jnp.zeros_like(fl_s)
    md_s[...] = jnp.zeros_like(md_s)
    for cp in copies[:10]:
        cp.wait()

    half = 0.5 * time_step
    pos = d_s[...] + time_step * v_s[...] + (half * time_step) * a_s[...]
    d_s[...] = pos
    v_s[...] = v_s[...] + half * a_s[...]
    pos_copies = [
        pltpu.make_async_copy(d_s.at[pl.ds(c, 1)], pos_out.at[c], out_sem.at[c])
        for c in range(3)
    ]
    for cp in pos_copies:
        cp.start()

    for x in range(NX):
        nf[3 * x : 3 * x + 3, 0:PLANE] = d_s[:, PLANE * x : PLANE * (x + 1)]
    planes = nf[...]
    blocks = [planes[:, :SPAN]] + [
        pltpu.roll(planes, WIDE - STEP * g, 1)[:, :SPAN] for g in range(1, GROUPS)
    ]
    rows = jnp.concatenate(blocks, axis=0)
    select = select_ref[...]
    lifted = dots(select, rows, ((1,), (1,)), False)

    corner = node_s[0:1, :].astype(jnp.float32)
    x0 = jnp.floor((corner + 0.5) * (1.0 / PLANE))
    rem = corner - PLANE * x0
    y0 = jnp.floor((rem + 0.5) * (1.0 / NZ))
    z0 = rem - NZ * y0
    grp = jnp.floor((y0 + 0.5) * (1.0 / (4 * GROUP)))
    low = (y0 - 4 * GROUP * grp) * 0.25 + GROUP * (z0 * 0.25)
    sub = lax.broadcasted_iota(jnp.int32, (SUB, 128), 0).astype(jnp.float32)
    mask = jnp.where(sub == low, 1.0, 0.0)[None]

    iota = lax.broadcasted_iota(jnp.int32, (GROUPS * GROW, 128), 0).astype(jnp.float32)
    goal = grp * GROW + 3.0 * x0
    picks = jnp.concatenate(
        [
            jnp.where(iota == goal + (3.0 * a + c), 1.0, 0.0).astype(jnp.bfloat16)
            for c in range(3)
            for a in range(5)
        ],
        axis=1,
    )
    gathered = dots(lifted, picks, ((1,), (0,)), True)
    for c in range(3):
        for a in range(5):
            j = (c * 5 + a) * 128
            part = gathered[:, j : j + 128].reshape(25, SUB, 128) * mask
            u_s[a * 32 : a * 32 + 25, c * 128 : (c + 1) * 128] = jnp.sum(part, axis=1)

    highest = lax.Precision.HIGHEST
    local = jnp.dot(
        deriv_ref[...], u_s[...], precision=highest, preferred_element_type=jnp.float32
    )
    for cp in copies[10:]:
        cp.wait()
    grads = [
        [local[l * 128 : l * 128 + 125, c * 128 : (c + 1) * 128] for c in range(3)]
        for l in range(3)
    ]
    maps = [[inv_s[INV_ROWS(3 * l + j)] for j in range(3)] for l in range(3)]
    weight = jac_s[...]
    lam = lame_s[...]
    mu = shear_s[...]
    h = [
        [sum(grads[l][c] * maps[l][j] for l in range(3)) for j in range(3)] for c in range(3)
    ]
    div = lam * (h[0][0] + h[1][1] + h[2][2])
    stress = [[None] * 3 for _ in range(3)]
    for c in range(3):
        for j in range(c, 3):
            s = mu * (h[c][j] + h[j][c])
            if c == j:
                s = s + div
            s = s * weight
            stress[c][j] = s
            stress[j][c] = s
    for l in range(3):
        for c in range(3):
            fl_s[l * 128 : l * 128 + 125, c * 128 : (c + 1) * 128] = sum(
                stress[c][j] * maps[l][j] for j in range(3)
            )
    md_s[0:125, :] = dens_s[...] * weight
    terms = jnp.dot(
        back_ref[...], fl_s[...], precision=highest, preferred_element_type=jnp.float32
    )
    heavy = jnp.dot(
        spread_ref[...], md_s[...], precision=highest, preferred_element_type=jnp.float32
    )

    spread_out = []
    puts = []
    iota2 = lax.broadcasted_iota(jnp.int32, (GROUPS * SROW, 128), 0).astype(jnp.float32)
    goal2 = grp * SROW + 4.0 * x0
    for k in range(4):
        for a in range(5):
            part = terms[a * 32 : a * 32 + 25, k * 128 : (k + 1) * 128] if k < 3 else heavy[a * 32 : a * 32 + 25]
            spread_out.append((part[:, None, :] * mask).reshape(25 * SUB, 128))
            puts.append(
                jnp.where(iota2 == goal2 + (4.0 * a + k), 1.0, 0.0).astype(jnp.bfloat16)
            )
    zp_s[...] = dots(
        jnp.concatenate(spread_out, axis=1),
        jnp.concatenate(puts, axis=1),
        ((1,), (1,)),
        True,
    )

    peers = sum(flag.astype(jnp.int32) for flag in has_low + has_high)
    pl.semaphore_wait(barrier, peers)

    def exchange(axis, send, recv):
        name, spot = names[axis], spots[axis]

        def copy(side, peer):
            return pltpu.make_async_remote_copy(
                src_ref=send.at[side],
                dst_ref=recv.at[1 - side],
                send_sem=send_sem.at[2 * axis + side],
                recv_sem=recv_sem.at[2 * axis + 1 - side],
                device_id={name: peer},
                device_id_type=MESH,
            )

        @pl.when(has_low[axis])
        def _():
            copy(0, spot - 1).start()

        @pl.when(has_high[axis])
        def _():
            copy(1, spot + 1).start()

        def finish(side):
            copy(1 - side, spot).wait_recv()

        def drain():
            for side, ok in ((0, has_low[axis]), (1, has_high[axis])):

                @pl.when(ok)
                def _():
                    copy(side, spot).wait_send()

        return finish, drain

    drains = []
    for b in range(5):
        z_send[0, b * 4 : b * 4 + 4] = zp_s[b * 5 * SUB : b * 5 * SUB + GROUP]
        top = (b * 5 + 4) * SUB + (EZ - 1) * GROUP
        z_send[1, b * 4 : b * 4 + 4] = zp_s[top : top + GROUP]
    finish, drain = exchange(0, z_send, z_recv)
    drains.append(drain)

    @pl.when(has_low[0])
    def _():
        finish(0)
        for b in range(5):
            at = b * 5 * SUB
            zp_s[at : at + GROUP] += z_recv[0, b * 4 : b * 4 + 4]

    @pl.when(has_high[0])
    def _():
        finish(1)
        for b in range(5):
            at = (b * 5 + 4) * SUB + (EZ - 1) * GROUP
            zp_s[at : at + GROUP] += z_recv[1, b * 4 : b * 4 + 4]

    flat = dots(zp_s[...], select, ((0,), (0,)), True)
    total = None
    blank = jnp.zeros((SROW, WIDE - SPAN), jnp.float32)
    for g in range(GROUPS):
        piece = jnp.concatenate([flat[g * SROW : (g + 1) * SROW], blank], axis=1)
        if g:
            piece = pltpu.roll(piece, STEP * g, 1)
        total = piece if total is None else total + piece
    grid_s[...] = total

    edge = WIDE - 128
    shift = PLANE - NZ - edge
    lanes = lax.broadcasted_iota(jnp.int32, (SROW, 128), 1)
    y_send[0] = grid_s[:, 0:128]
    y_send[1] = grid_s[:, edge:WIDE]
    finish, drain = exchange(1, y_send, y_recv)
    drains.append(drain)

    @pl.when(has_low[1])
    def _():
        finish(0)
        got = pltpu.roll(y_recv[0], 128 - shift, 1)
        grid_s[:, 0:128] += jnp.where(lanes < NZ, got, 0.0)

    @pl.when(has_high[1])
    def _():
        finish(1)
        got = jnp.where(lanes < NZ, y_recv[1], 0.0)
        grid_s[:, edge:WIDE] += pltpu.roll(got, shift, 1)

    x_send[0] = grid_s[0:8]
    x_send[1] = grid_s[SROW - 8 : SROW]
    finish, drain = exchange(2, x_send, x_recv)
    drains.append(drain)

    @pl.when(has_low[2])
    def _():
        finish(0)
        grid_s[0:4] += x_recv[0, 0:4]

    @pl.when(has_high[2])
    def _():
        finish(1)
        grid_s[SROW - 8 : SROW - 4] += x_recv[1, 0:4]

    for x in range(NX):
        force = grid_s[4 * x : 4 * x + 3, 0:PLANE]
        mass = grid_s[4 * x + 3 : 4 * x + 4, 0:PLANE]
        acc_s[:, PLANE * x : PLANE * (x + 1)] = force / mass
    v_s[...] = v_s[...] + half * acc_s[...]
    last = []
    for k, (src, dst) in enumerate(((v_s, spd_out), (acc_s, acc_out))):
        for c in range(3):
            last.append(
                pltpu.make_async_copy(
                    src.at[pl.ds(c, 1)], dst.at[c], out_sem.at[3 + 3 * k + c]
                )
            )
    for cp in last:
        cp.start()
    for drain in drains:
        drain()
    for cp in pos_copies + last:
        cp.wait()


def ELEM_SRC(ref):
    return ref


def INV_ROWS(k):
    return (k,)


def body(displ, veloc, accel, node_index, inv_map, jac_weight, lame_first, shear_mod, density):
    nodes = displ.shape[4]
    elements = node_index.shape[4]
    select, deriv, back, spread = constants()
    fields = [x.reshape(3, 1, nodes) for x in (displ, veloc, accel)]
    elems = [
        x.reshape(125, elements) for x in (jac_weight, lame_first, shear_mod, density)
    ]
    hbm = pl.BlockSpec(memory_space=pl.ANY)
    vmem = pl.BlockSpec(memory_space=pltpu.VMEM)
    f32 = jnp.float32
    out = jax.ShapeDtypeStruct((3, 1, nodes), f32)
    elem = pltpu.VMEM((125, elements), f32)
    width = GROUPS * SROW
    outs = pl.pallas_call(
        kernel,
        out_shape=(out, out, out),
        in_specs=[hbm] * 9 + [vmem] * 4,
        out_specs=(hbm, hbm, hbm),
        scratch_shapes=[
            pltpu.VMEM((3, nodes), f32),
            pltpu.VMEM((3, nodes), f32),
            pltpu.VMEM((3, nodes), f32),
            pltpu.VMEM((125, elements), jnp.int32),
            pltpu.VMEM((9, 125, elements), f32),
            elem, elem, elem, elem,
            pltpu.VMEM((GROW, WIDE), f32),
            pltpu.VMEM((160, 384), f32),
            pltpu.VMEM((384, 384), f32),
            pltpu.VMEM((128, 128), f32),
            pltpu.VMEM((25 * SUB, width), f32),
            pltpu.VMEM((SROW, WIDE), f32),
            pltpu.VMEM((3, nodes), f32),
            pltpu.VMEM((2, 24, width), f32),
            pltpu.VMEM((2, 24, width), f32),
            pltpu.VMEM((2, SROW, 128), f32),
            pltpu.VMEM((2, SROW, 128), f32),
            pltpu.VMEM((2, 8, WIDE), f32),
            pltpu.VMEM((2, 8, WIDE), f32),
            pltpu.SemaphoreType.DMA((15,)),
            pltpu.SemaphoreType.DMA((9,)),
            pltpu.SemaphoreType.DMA((6,)),
            pltpu.SemaphoreType.DMA((6,)),
        ],
        compiler_params=pltpu.CompilerParams(collective_id=0, has_side_effects=True),
    )(
        *fields,
        node_index.reshape(125, elements),
        inv_map.reshape(9, 125, elements),
        *elems,
        jnp.asarray(select, jnp.bfloat16),
        jnp.asarray(deriv),
        jnp.asarray(back),
        jnp.asarray(spread),
    )
    shape = (3, 1, 1, 1, nodes)
    return tuple(x.reshape(shape) for x in outs)


def solution(mesh):
    field = P(None, "gx", "gy", "gz", None)
    elem = P("gx", "gy", "gz", None, None)
    placed = (field,) * 3 + (elem, P("gx", "gy", "gz", None, None, None)) + (elem,) * 4
    return jax.shard_map(
        body, mesh=mesh, in_specs=placed, out_specs=(field,) * 3, check_vma=False
    )
```

```python
import jax
import jax.numpy as jnp
import numpy as np
from jax import lax
from jax.experimental import pallas as pl
from jax.experimental.pallas import tpu as pltpu
from jax.sharding import PartitionSpec as P

EX = 4
EY = 16
EZ = 2
NX = 4 * EX + 1
NY = 4 * EY + 1
NZ = 4 * EZ + 1
PLANE = NY * NZ
GROUP = 4
GROUPS = EY // GROUP
STEP = 4 * GROUP * NZ
SPAN = 256
WIDE = 640
GROW = 64
SROW = 72
SUB = EZ * GROUP

time_step = 0.1
MESH = pl.DeviceIdType.MESH


def derivative_table():
    points = np.array([-1.0, -np.sqrt(3.0 / 7.0), 0.0, np.sqrt(3.0 / 7.0), 1.0])
    count = points.shape[0]
    weights = np.array(
        [
            1.0 / np.prod([points[s] - points[o] for o in range(count) if o != s])
            for s in range(count)
        ]
    )
    table = np.zeros((count, count))
    for t in range(count):
        for s in range(count):
            if t != s:
                table[t, s] = weights[s] / weights[t] / (points[t] - points[s])
        table[t, t] = -np.sum(table[t])
    return table


def constants():
    table = derivative_table()
    select = np.zeros((25 * SUB, SPAN), np.float32)
    for b in range(5):
        for c in range(5):
            for ez in range(EZ):
                for ey in range(GROUP):
                    row = (b * 5 + c) * SUB + ez * GROUP + ey
                    select[row, (4 * ey + b) * NZ + 4 * ez + c] = 1.0
    eye = np.eye(5)
    parts = [
        np.kron(table, np.kron(eye, eye)),
        np.kron(eye, np.kron(table, eye)),
        np.kron(eye, np.kron(eye, table)),
    ]
    pad = np.zeros((125, 160))
    for a in range(5):
        for q in range(25):
            pad[a * 25 + q, a * 32 + q] = 1.0
    deriv = np.zeros((384, 160), np.float32)
    for l in range(3):
        deriv[l * 128 : l * 128 + 125] = parts[l] @ pad
    spread = np.zeros((160, 128), np.float32)
    spread[:, :125] = pad.T
    return select, deriv, -deriv.T.copy(), spread


def split3(x):
    hi = x.astype(jnp.bfloat16)
    rest = x - hi.astype(jnp.float32)
    mid = rest.astype(jnp.bfloat16)
    low = (rest - mid.astype(jnp.float32)).astype(jnp.bfloat16)
    return (hi, mid, low)


def dots(x, y, dims, split_left):
    total = None
    for piece in split3(x if split_left else y):
        left, right = (piece, y) if split_left else (x, piece)
        out = lax.dot_general(
            left, right, (dims, ((), ())), preferred_element_type=jnp.float32
        )
        total = out if total is None else total + out
    return total


def squeezed(ref):
    return ref.at[:, 0] if len(ref.shape) == 3 else ref.at[:, :, 0]


def kernel(
    displ, veloc, accel, node, inv, jac, lame, shear, dens,
    select_ref, deriv_ref, back_ref, spread_ref,
    acc_out,
    d_s, v_s, a_s, node_s, inv_s, jac_s, lame_s, shear_s, dens_s,
    nf, u_s, fl_s, md_s, zp_s, grid_s, acc_s,
    z_send, z_recv, y_send, y_recv, x_send, x_recv,
    in_sem, out_sem, send_sem, recv_sem,
):
    names = ("gz", "gy", "gx")
    spots = [lax.axis_index(n) for n in names]
    sizes = [lax.axis_size(n) for n in names]
    has_low = [s > 0 for s in spots]
    has_high = [s < n - 1 for s, n in zip(spots, sizes)]
    barrier = pltpu.get_barrier_semaphore()
    for n, s, lo, hi in zip(names, spots, has_low, has_high):

        @pl.when(lo)
        def _():
            pl.semaphore_signal(barrier, inc=1, device_id={n: s - 1}, device_id_type=MESH)

        @pl.when(hi)
        def _():
            pl.semaphore_signal(barrier, inc=1, device_id={n: s + 1}, device_id_type=MESH)

    copies = []
    for k, (src, dst) in enumerate(((displ, d_s), (veloc, v_s), (accel, a_s))):
        for c in range(3):
            copies.append(
                pltpu.make_async_copy(
                    src.at[c], dst.at[pl.ds(c, 1)], in_sem.at[3 * k + c]
                )
            )
    elems = ((node, node_s), (inv, inv_s), (jac, jac_s), (lame, lame_s), (shear, shear_s), (dens, dens_s))
    for k, (src, dst) in enumerate(elems):
        copies.append(pltpu.make_async_copy(squeezed(src), dst, in_sem.at[9 + k]))
    for cp in copies:
        cp.start()
    nf[...] = jnp.zeros_like(nf)
    u_s[...] = jnp.zeros_like(u_s)
    fl_s[...] = jnp.zeros_like(fl_s)
    md_s[...] = jnp.zeros_like(md_s)
    for cp in copies[:10]:
        cp.wait()

    half = 0.5 * time_step
    pos = d_s[...] + time_step * v_s[...] + (half * time_step) * a_s[...]
    d_s[...] = pos
    for x in range(NX):
        nf[3 * x : 3 * x + 3, 0:PLANE] = d_s[:, PLANE * x : PLANE * (x + 1)]
    planes = nf[...]
    blocks = [planes[:, :SPAN]] + [
        pltpu.roll(planes, WIDE - STEP * g, 1)[:, :SPAN] for g in range(1, GROUPS)
    ]
    rows = jnp.concatenate(blocks, axis=0)
    select = select_ref[...]
    lifted = dots(select, rows, ((1,), (1,)), False)

    corner = node_s[0:1, :].astype(jnp.float32)
    x0 = jnp.floor((corner + 0.5) * (1.0 / PLANE))
    rem = corner - PLANE * x0
    y0 = jnp.floor((rem + 0.5) * (1.0 / NZ))
    z0 = rem - NZ * y0
    grp = jnp.floor((y0 + 0.5) * (1.0 / (4 * GROUP)))
    low = (y0 - 4 * GROUP * grp) * 0.25 + GROUP * (z0 * 0.25)
    sub = lax.broadcasted_iota(jnp.int32, (SUB, 128), 0).astype(jnp.float32)
    mask = jnp.where(sub == low, 1.0, 0.0)[None]

    iota = lax.broadcasted_iota(jnp.int32, (GROUPS * GROW, 128), 0).astype(jnp.float32)
    goal = grp * GROW + 3.0 * x0
    picks = jnp.concatenate(
        [
            jnp.where(iota == goal + (3.0 * a + c), 1.0, 0.0).astype(jnp.bfloat16)
            for c in range(3)
            for a in range(5)
        ],
        axis=1,
    )
    gathered = dots(lifted, picks, ((1,), (0,)), True)
    for c in range(3):
        for a in range(5):
            j = (c * 5 + a) * 128
            part = gathered[:, j : j + 128].reshape(25, SUB, 128) * mask
            u_s[a * 32 : a * 32 + 25, c * 128 : (c + 1) * 128] = jnp.sum(part, axis=1)

    highest = lax.Precision.HIGHEST
    local = jnp.dot(
        deriv_ref[...], u_s[...], precision=highest, preferred_element_type=jnp.float32
    )
    for cp in copies[10:]:
        cp.wait()
    grads = [
        [local[l * 128 : l * 128 + 125, c * 128 : (c + 1) * 128] for c in range(3)]
        for l in range(3)
    ]
    maps = [[inv_s[3 * l + j] for j in range(3)] for l in range(3)]
    weight = jac_s[...]
    lam = lame_s[...]
    mu = shear_s[...]
    h = [
        [sum(grads[l][c] * maps[l][j] for l in range(3)) for j in range(3)] for c in range(3)
    ]
    div = lam * (h[0][0] + h[1][1] + h[2][2])
    stress = [[None] * 3 for _ in range(3)]
    for c in range(3):
        for j in range(c, 3):
            s = mu * (h[c][j] + h[j][c])
            if c == j:
                s = s + div
            s = s * weight
            stress[c][j] = s
            stress[j][c] = s
    for l in range(3):
        for c in range(3):
            fl_s[l * 128 : l * 128 + 125, c * 128 : (c + 1) * 128] = sum(
                stress[c][j] * maps[l][j] for j in range(3)
            )
    md_s[0:125, :] = dens_s[...] * weight
    terms = jnp.dot(
        back_ref[...], fl_s[...], precision=highest, preferred_element_type=jnp.float32
    )
    heavy = jnp.dot(
        spread_ref[...], md_s[...], precision=highest, preferred_element_type=jnp.float32
    )

    spread_out = []
    puts = []
    iota2 = lax.broadcasted_iota(jnp.int32, (GROUPS * SROW, 128), 0).astype(jnp.float32)
    goal2 = grp * SROW + 4.0 * x0
    for k in range(4):
        for a in range(5):
            part = terms[a * 32 : a * 32 + 25, k * 128 : (k + 1) * 128] if k < 3 else heavy[a * 32 : a * 32 + 25]
            spread_out.append((part[:, None, :] * mask).reshape(25 * SUB, 128))
            puts.append(
                jnp.where(iota2 == goal2 + (4.0 * a + k), 1.0, 0.0).astype(jnp.bfloat16)
            )
    zp_s[...] = dots(
        jnp.concatenate(spread_out, axis=1),
        jnp.concatenate(puts, axis=1),
        ((1,), (1,)),
        True,
    )

    peers = sum(flag.astype(jnp.int32) for flag in has_low + has_high)
    pl.semaphore_wait(barrier, peers)

    def exchange(axis, send, recv):
        name, spot = names[axis], spots[axis]

        def copy(side, peer):
            return pltpu.make_async_remote_copy(
                src_ref=send.at[side],
                dst_ref=recv.at[1 - side],
                send_sem=send_sem.at[2 * axis + side],
                recv_sem=recv_sem.at[2 * axis + 1 - side],
                device_id={name: peer},
                device_id_type=MESH,
            )

        @pl.when(has_low[axis])
        def _():
            copy(0, spot - 1).start()

        @pl.when(has_high[axis])
        def _():
            copy(1, spot + 1).start()

        def finish(side):
            copy(1 - side, spot).wait_recv()

        def drain():
            for side, ok in ((0, has_low[axis]), (1, has_high[axis])):

                @pl.when(ok)
                def _():
                    copy(side, spot).wait_send()

        return finish, drain

    drains = []
    for b in range(5):
        z_send[0, b * 4 : b * 4 + 4] = zp_s[b * 5 * SUB : b * 5 * SUB + GROUP]
        top = (b * 5 + 4) * SUB + (EZ - 1) * GROUP
        z_send[1, b * 4 : b * 4 + 4] = zp_s[top : top + GROUP]
    finish, drain = exchange(0, z_send, z_recv)
    drains.append(drain)

    @pl.when(has_low[0])
    def _():
        finish(0)
        for b in range(5):
            at = b * 5 * SUB
            zp_s[at : at + GROUP] += z_recv[0, b * 4 : b * 4 + 4]

    @pl.when(has_high[0])
    def _():
        finish(1)
        for b in range(5):
            at = (b * 5 + 4) * SUB + (EZ - 1) * GROUP
            zp_s[at : at + GROUP] += z_recv[1, b * 4 : b * 4 + 4]

    flat = dots(zp_s[...], select, ((0,), (0,)), True)
    total = None
    blank = jnp.zeros((SROW, WIDE - SPAN), jnp.float32)
    for g in range(GROUPS):
        piece = jnp.concatenate([flat[g * SROW : (g + 1) * SROW], blank], axis=1)
        if g:
            piece = pltpu.roll(piece, STEP * g, 1)
        total = piece if total is None else total + piece
    grid_s[...] = total

    edge = WIDE - 128
    shift = PLANE - NZ - edge
    lanes = lax.broadcasted_iota(jnp.int32, (SROW, 128), 1)
    y_send[0] = grid_s[:, 0:128]
    y_send[1] = grid_s[:, edge:WIDE]
    finish, drain = exchange(1, y_send, y_recv)
    drains.append(drain)

    @pl.when(has_low[1])
    def _():
        finish(0)
        got = pltpu.roll(y_recv[0], 128 - shift, 1)
        grid_s[:, 0:128] += jnp.where(lanes < NZ, got, 0.0)

    @pl.when(has_high[1])
    def _():
        finish(1)
        got = jnp.where(lanes < NZ, y_recv[1], 0.0)
        grid_s[:, edge:WIDE] += pltpu.roll(got, shift, 1)

    x_send[0] = grid_s[0:8]
    x_send[1] = grid_s[SROW - 8 : SROW]
    finish, drain = exchange(2, x_send, x_recv)
    drains.append(drain)

    @pl.when(has_low[2])
    def _():
        finish(0)
        grid_s[0:4] += x_recv[0, 0:4]

    @pl.when(has_high[2])
    def _():
        finish(1)
        grid_s[SROW - 8 : SROW - 4] += x_recv[1, 0:4]

    for x in range(NX):
        force = grid_s[4 * x : 4 * x + 3, 0:PLANE]
        mass = grid_s[4 * x + 3 : 4 * x + 4, 0:PLANE]
        acc_s[:, PLANE * x : PLANE * (x + 1)] = force / mass
    last = [
        pltpu.make_async_copy(acc_s.at[pl.ds(c, 1)], acc_out.at[c], out_sem.at[c])
        for c in range(3)
    ]
    for cp in last:
        cp.start()
    for drain in drains:
        drain()
    for cp in last:
        cp.wait()


def body(displ, veloc, accel, node_index, inv_map, jac_weight, lame_first, shear_mod, density):
    nodes = displ.shape[4]
    elements = node_index.shape[4]
    select, deriv, back, spread = constants()
    fields = [x.reshape(3, 1, nodes) for x in (displ, veloc, accel)]
    elems = [
        x.reshape(125, 1, elements) for x in (jac_weight, lame_first, shear_mod, density)
    ]
    hbm = pl.BlockSpec(memory_space=pl.ANY)
    vmem = pl.BlockSpec(memory_space=pltpu.VMEM)
    f32 = jnp.float32
    out = jax.ShapeDtypeStruct((3, 1, nodes), f32)
    elem = pltpu.VMEM((125, elements), f32)
    width = GROUPS * SROW
    result = pl.pallas_call(
        kernel,
        out_shape=out,
        in_specs=[hbm] * 9 + [vmem] * 4,
        out_specs=hbm,
        scratch_shapes=[
            pltpu.VMEM((3, nodes), f32),
            pltpu.VMEM((3, nodes), f32),
            pltpu.VMEM((3, nodes), f32),
            pltpu.VMEM((125, elements), jnp.int32),
            pltpu.VMEM((9, 125, elements), f32),
            elem, elem, elem, elem,
            pltpu.VMEM((GROW, WIDE), f32),
            pltpu.VMEM((160, 384), f32),
            pltpu.VMEM((384, 384), f32),
            pltpu.VMEM((128, 128), f32),
            pltpu.VMEM((25 * SUB, width), f32),
            pltpu.VMEM((SROW, WIDE), f32),
            pltpu.VMEM((3, nodes), f32),
            pltpu.VMEM((2, 24, width), f32),
            pltpu.VMEM((2, 24, width), f32),
            pltpu.VMEM((2, SROW, 128), f32),
            pltpu.VMEM((2, SROW, 128), f32),
            pltpu.VMEM((2, 8, WIDE), f32),
            pltpu.VMEM((2, 8, WIDE), f32),
            pltpu.SemaphoreType.DMA((15,)),
            pltpu.SemaphoreType.DMA((3,)),
            pltpu.SemaphoreType.DMA((6,)),
            pltpu.SemaphoreType.DMA((6,)),
        ],
        compiler_params=pltpu.CompilerParams(collective_id=0, has_side_effects=True),
    )(
        *fields,
        node_index.reshape(125, 1, elements),
        inv_map.reshape(9, 125, 1, elements),
        *elems,
        jnp.asarray(select, jnp.bfloat16),
        jnp.asarray(deriv),
        jnp.asarray(back),
        jnp.asarray(spread),
    )
    half = 0.5 * time_step
    acceleration = result.reshape(displ.shape)
    position = displ + time_step * veloc + (half * time_step) * accel
    speed = veloc + half * accel + half * acceleration
    return (position, speed, acceleration)


def solution(mesh):
    field = P(None, "gx", "gy", "gz", None)
    elem = P("gx", "gy", "gz", None, None)
    placed = (field,) * 3 + (elem, P("gx", "gy", "gz", None, None, None)) + (elem,) * 4
    return jax.shard_map(
        body, mesh=mesh, in_specs=placed, out_specs=(field,) * 3, check_vma=False
    )
```
